32 devices in a mesh: leaf: 8 (over y, x, core), rows: 4 (over z).
Axes of the slice: x: 2, y: 2, z: 4, core: 2. Of those that a mesh axis runs over, the one named last changes fastest.
Arguments:
- right_side: float32 [8, 96, 2048], P('leaf', None, 'rows'), may hold values from -6 to 6
- diag_inverse: float32 [8, 2048, 2048], P('leaf', 'rows')
- lower_blocks: float32 [8, 2048, 2048], P('leaf', 'rows'), may hold values from -0.125 to 0.125
- block_pattern: int32 [8, 32, 32], P('leaf', 'rows'), may hold values 0 or 1
Outputs:
- solution: float32 [8, 96, 2048], P('leaf', None, 'rows')
- ancestor_update: float32 [8, 96, 2048], P('leaf', None, 'rows')
The draws below stay inside these ranges and needn't reach their ends.
All inputs are finite; a program needn't handle non-finite values. No bound on the sum of `block_pattern` on one device may be relied on, other than what follows from the above.
Results may differ from the reference program's by a relative error of at most 0.00017.
Values sent between devices are 32-bit elements; how exact they have to be, the bound alone decides.
A program may use at most 64 MiB of HBM per device.

```python
import jax
import jax.numpy as jnp
from jax import lax

W = 2048
BLK = 64
NBLK = 32
SOURCES = 96
GROUPS = 8


def draw_diag_inverse(key, part):
    first_key, second_key = jax.random.split(jax.random.fold_in(key, 17))
    diagonal_part = jax.random.uniform(first_key, (GROUPS, W), jnp.float32, 0.5, 1.5)
    spread = jax.random.normal(second_key, (GROUPS, W, W), jnp.float32)
    strict = jnp.tril(spread, -1) * W ** (-0.5)
    return strict + diagonal_part[:, :, None] * jnp.eye(W, dtype=jnp.float32)[None]


def place_ends(array, stream_key, low, largest):
    place = [jax.random.randint(jax.random.fold_in(stream_key, axis), (), 0, length) for axis, length in enumerate(array.shape)]
    widest = array.shape.index(max(array.shape))
    neighbour = place[:widest] + [(place[widest] + 1) % array.shape[widest]] + place[widest + 1:]
    return array.at[tuple(place)].set(low).at[tuple(neighbour)].set(largest)


def level_of(rng, shape, shards, least, largest):
    loudness, own = 1.0, jax.random.fold_in(rng, 6)
    for position, blocks in shards:
        heights = jnp.exp(jax.random.uniform(jax.random.fold_in(own, position), (blocks,), jnp.float32, least / len(shards), largest / len(shards)))
        loudness = loudness * jnp.repeat(heights, shape[position] // blocks).reshape([-1 if axis == position else 1 for axis in range(len(shape))])
    return loudness


def normal_values(own_key, extent, deviation, reach, cuts=(), kind=jnp.bfloat16):
    values = deviation * jax.random.normal(own_key, extent, jnp.float32)
    if cuts:
        values = values * level_of(own_key, extent, cuts, -0.22, 0.18)
    return jnp.clip(values, -reach, reach).astype(kind)


def setup_inputs(seed: int = 0) -> dict:
    arg_keys = jax.random.split(jax.random.key(seed), 5)
    return {
        "right_side": normal_values(arg_keys[0], (GROUPS, SOURCES, W), 1.0, 6.0, ((0, 8), (2, 4)), jnp.float32),
        "diag_inverse": draw_diag_inverse(jax.random.fold_in(arg_keys[4], 71), 0),
        "lower_blocks": normal_values(arg_keys[2], (GROUPS, W, W), W ** -0.5, 0.125, ((0, 8), (1, 4)), jnp.float32),
        "block_pattern": place_ends((jax.random.randint(arg_keys[3], (GROUPS, NBLK, NBLK), 0, 5) < 3).astype(jnp.int32), jax.random.fold_in(arg_keys[3], 1), 0, 1),
    }


def reference(right_side, diag_inverse, lower_blocks, block_pattern):
    def advance(incoming, items):
        sources, inverse, values, pattern = items
        expanded = jnp.repeat(jnp.repeat(pattern.astype(jnp.float32), BLK, 0), BLK, 1)
        solved = jnp.dot(sources - incoming, inverse.T, precision=lax.Precision.HIGHEST, preferred_element_type=jnp.float32)
        update = jnp.dot(solved, (values * expanded).T, precision=lax.Precision.HIGHEST, preferred_element_type=jnp.float32)
        return update, (solved, update)

    start_update = jnp.zeros((SOURCES, W), jnp.float32)
    _, (solution, ancestor_update) = lax.scan(advance, start_update, (right_side, diag_inverse, lower_blocks, block_pattern))
    return solution, ancestor_update
```

```python
import functools

import jax
import jax.numpy as jnp
from jax import lax
from jax.experimental import pallas as pl
from jax.experimental.pallas import tpu as pltpu
from jax.sharding import PartitionSpec as P

MESH = pl.DeviceIdType.MESH
WAVE = 8
AHEAD = 1
FIRST_AHEAD = 1
EARLY = 3
HELPER = 2
VMEM_LIMIT = 60000000
LANES = 128


def partner(place, step, size):
    if size & (size - 1):
        return (place + step) % size
    result, bit = 0, 1
    while bit < size:
        result = result + ((place // bit + step // bit) % 2) * bit
        bit *= 2
    return result


def halves(x):
    high = x.astype(jnp.bfloat16)
    low = (x - high.astype(jnp.float32)).astype(jnp.bfloat16)
    return high, low


def kernel(
    groups, splits, right_ref, inverse_hbm, lower_hbm, pattern_ref, solved_ref, update_ref,
    inverse_stage, lower_stage, inverse_parts, lower_parts, arriving, gathered, leaving, next_right, detour,
    inverse_sem, lower_sem, arriving_sem, gathered_sem, first_sem, leaving_sem, spread_sem, right_sem, detour_sem, passed_sem,
):
    g = lax.axis_index("leaf")
    z = lax.axis_index("rows")
    waves, size, local = right_ref.shape
    width = pattern_ref.shape[1]
    pieces = inverse_sem.shape[0]
    piece = local // pieces
    total = splits * local
    helped = groups > HELPER and splits > 1 and waves > EARLY
    direct = EARLY if helped else waves
    ahead = AHEAD + (FIRST_AHEAD - AHEAD) * (1 - jnp.minimum(g, 1))

    def piece_copies(source, stage, sems):
        return [
            pltpu.make_async_copy(
                source.at[pl.ds(i * piece, piece)], stage.at[pl.ds(i * piece, piece)], sems.at[i]
            )
            for i in range(pieces)
        ]

    inverse_copies = piece_copies(inverse_hbm, inverse_stage, inverse_sem)
    lower_copies = piece_copies(lower_hbm, lower_stage, lower_sem)
    for copy in inverse_copies:
        copy.start()

    barrier = pltpu.get_barrier_semaphore()

    def greet(leaf, row):
        pl.semaphore_signal(
            barrier, inc=1, device_id={"leaf": leaf, "rows": row}, device_id_type=MESH
        )

    for j in range(1, splits):
        greet(g, partner(z, j, splits))

    @pl.when(g > 0)
    def _():
        for j in range(splits):
            greet(g - 1, partner(z, j, splits))

    @pl.when(g < groups - 1)
    def _():
        for j in range(splits):
            greet(g + 1, partner(z, j, splits))

    neighbours = jnp.minimum(g, 1) + jnp.minimum(groups - 1 - g, 1)
    if helped:
        for one, other in ((0, HELPER), (HELPER, 0)):
            @pl.when(g == one)
            def _(other=other):
                for j in range(splits):
                    greet(other, partner(z, j, splits))

        neighbours = neighbours + jnp.where((g == 0) | (g == HELPER), 1, 0)
    pl.semaphore_wait(barrier, splits - 1 + splits * neighbours)

    def right_copy():
        return pltpu.make_async_remote_copy(
            src_ref=right_ref, dst_ref=next_right, send_sem=right_sem.at[0],
            recv_sem=right_sem.at[1], device_id={"leaf": g - 1, "rows": z}, device_id_type=MESH,
        )

    def first_copy(k, j):
        return pltpu.make_async_remote_copy(
            src_ref=right_ref.at[k], dst_ref=arriving.at[k, z], send_sem=first_sem.at[k, j],
            recv_sem=arriving_sem.at[k, z],
            device_id={"leaf": g, "rows": partner(z, j, splits)}, device_id_type=MESH,
        )

    def own_copy(k):
        return pltpu.make_async_copy(right_ref.at[k], arriving.at[k, z], arriving_sem.at[k, z])

    def onward_copy(k, j):
        return pltpu.make_async_remote_copy(
            src_ref=leaving.at[k], dst_ref=arriving.at[k, z], send_sem=leaving_sem.at[k, j],
            recv_sem=arriving_sem.at[k, z],
            device_id={"leaf": g + 1, "rows": partner(z, j, splits)}, device_id_type=MESH,
        )

    def spread_copy(k, j):
        return pltpu.make_async_remote_copy(
            src_ref=gathered.at[k, z], dst_ref=gathered.at[k, z], send_sem=spread_sem.at[k, j],
            recv_sem=gathered_sem.at[k, z],
            device_id={"leaf": g, "rows": partner(z, j, splits)}, device_id_type=MESH,
        )

    def detour_copy():
        rest = pl.ds(direct, waves - direct)
        return pltpu.make_async_remote_copy(
            src_ref=right_ref.at[rest], dst_ref=detour.at[rest], send_sem=detour_sem.at[0],
            recv_sem=detour_sem.at[1], device_id={"leaf": HELPER, "rows": z}, device_id_type=MESH,
        )

    def passed_copy(k, j):
        return pltpu.make_async_remote_copy(
            src_ref=detour.at[k], dst_ref=arriving.at[k, z], send_sem=passed_sem.at[k, j],
            recv_sem=arriving_sem.at[k, z],
            device_id={"leaf": 0, "rows": partner(z, j, splits)}, device_id_type=MESH,
        )

    @pl.when(g == 0)
    def _():
        def direct_sends(k, _):
            for j in range(splits - 1, 0, -1):
                first_copy(k, j).start()
            return 0

        def own_sends(k, _):
            own_copy(k).start()
            return 0

        direct_sends(0, 0)
        own_copy(0).start()
        if helped:
            detour_copy().start()
        lax.fori_loop(1, direct, direct_sends, 0)
        lax.fori_loop(1, waves, own_sends, 0)

    @pl.when(g > 0)
    def _():
        right_copy().start()

    def store_turned(parts, rows, q, values):
        high, low = halves(values.T)
        parts[q, :, pl.ds(rows, piece)] = high
        parts[q, :, pl.ds(local + rows, piece)] = low

    def prepare_inverse():
        for i in range(pieces):
            inverse_copies[i].wait()
            lower_copies[i].start()
            for q in range(splits):
                store_turned(
                    inverse_parts, i * piece, q,
                    inverse_stage[pl.ds(i * piece, piece), pl.ds(q * local, local)],
                )

    def prepare_lower():
        block = total // width
        row = lax.broadcasted_iota(jnp.int32, (width, total), 0)
        column = lax.broadcasted_iota(jnp.int32, (width, total), 1)
        spread = jnp.where(column // block == row, 1.0, 0.0).astype(jnp.bfloat16)
        mask = jnp.dot(
            pattern_ref[...].astype(jnp.float32).astype(jnp.bfloat16), spread,
            preferred_element_type=jnp.float32,
        )
        for i in range(pieces):
            lower_copies[i].wait()
            for q in range(splits):
                kept = [
                    lower_stage[pl.ds(h * block, block), pl.ds(q * local, local)]
                    * mask[h : h + 1, q * local : (q + 1) * local]
                    for h in range(i * piece // block, (i + 1) * piece // block)
                ]
                store_turned(lower_parts, i * piece, q, jnp.concatenate(kept, 0))

    def product(x, parts):
        high, low = halves(x)
        out = lax.dot_general(
            jnp.concatenate([high, low], 0), parts, (((1,), (0,)), ((), ())),
            preferred_element_type=jnp.float32,
        )
        return (out[:size, :local] + (out[size:, :local] + out[:size, local:])) + out[size:, local:]

    def solve(k):
        result = None
        for j in range(splits):
            q = partner(z, j, splits)
            pltpu.make_async_copy(arriving.at[k, q], arriving.at[k, q], arriving_sem.at[k, q]).wait()
            term = product(arriving[k, q], inverse_parts[q])
            result = term if result is None else result + term
        gathered[k, z] = result
        for j in range(splits - 1, 0, -1):
            spread_copy(k, j).start()
        solved_ref[k] = result

    def push(k):
        result = None
        for j in range(splits):
            q = partner(z, j, splits)
            if j:
                pltpu.make_async_copy(gathered.at[k, q], gathered.at[k, q], gathered_sem.at[k, q]).wait()
            term = product(gathered[k, q], lower_parts[q])
            result = term if result is None else result + term

        @pl.when(g < groups - 1)
        def _():
            leaving[k] = next_right[k] - result
            for j in range(splits - 1, -1, -1):
                onward_copy(k, j).start()

        update_ref[k] = result

    prepare_inverse()

    if helped:
        @pl.when(g == HELPER)
        def _():
            detour_copy().wait_recv()

            def pass_on(k, _):
                for j in range(splits - 1, 0, -1):
                    passed_copy(k, j).start()
                return 0

            lax.fori_loop(direct, waves, pass_on, 0)

    @pl.when(g > 0)
    def _():
        prepare_lower()

    def section(k, _):
        @pl.when(k < waves)
        def _():
            solve(k)

        @pl.when((k == 0) & (g == 0))
        def _():
            prepare_lower()

        @pl.when((k == ahead) & (g < groups - 1))
        def _():
            right_copy().wait_recv()

        @pl.when(k >= ahead)
        def _():
            push(k - ahead)

        return 0

    lax.fori_loop(0, waves + ahead, section, 0)

    def finish(k, _):
        for j in range(1, splits):
            spread_copy(k, j).wait_send()

        @pl.when((g == 0) & (k < direct))
        def _():
            for j in range(1, splits):
                first_copy(k, j).wait_send()

        if helped:
            @pl.when((g == HELPER) & (k >= direct))
            def _():
                for j in range(1, splits):
                    passed_copy(k, j).wait_send()

        @pl.when(g < groups - 1)
        def _():
            for j in range(splits):
                onward_copy(k, j).wait_send()

        return 0

    lax.fori_loop(0, waves, finish, 0)

    @pl.when(g > 0)
    def _():
        right_copy().wait_send()

    if helped:
        @pl.when(g == 0)
        def _():
            detour_copy().wait_send()


def place(solved_ref, update_ref, solved_hbm, update_hbm, sems):
    copies = [
        pltpu.make_async_copy(solved_ref, solved_hbm, sems.at[0]),
        pltpu.make_async_copy(update_ref, update_hbm, sems.at[1]),
    ]
    for copy in copies:
        copy.start()
    for copy in copies:
        copy.wait()


def on_device(groups, splits, right_side, diag_inverse, lower_blocks, block_pattern):
    _, sources, local = right_side.shape
    total = diag_inverse.shape[2]
    pieces = local // LANES
    waves = sources // WAVE
    VMEM = pl.BlockSpec(memory_space=pltpu.VMEM)
    ANY = pl.BlockSpec(memory_space=pl.ANY)
    shape = jax.ShapeDtypeStruct((waves, WAVE, local), jnp.float32)
    dma = pltpu.SemaphoreType.DMA
    solved, update = pl.pallas_call(
        functools.partial(kernel, groups, splits),
        out_shape=(shape, shape),
        in_specs=[VMEM, ANY, ANY, VMEM],
        out_specs=(VMEM, VMEM),
        scratch_shapes=[
            pltpu.VMEM((local, total), jnp.float32),
            pltpu.VMEM((local, total), jnp.float32),
            pltpu.VMEM((splits, local, 2 * local), jnp.bfloat16),
            pltpu.VMEM((splits, local, 2 * local), jnp.bfloat16),
            pltpu.VMEM((waves, splits, WAVE, local), jnp.float32),
            pltpu.VMEM((waves, splits, WAVE, local), jnp.float32),
            pltpu.VMEM((waves, WAVE, local), jnp.float32),
            pltpu.VMEM((waves, WAVE, local), jnp.float32),
            pltpu.VMEM((waves, WAVE, local), jnp.float32),
            dma((pieces,)),
            dma((pieces,)),
            dma((waves, splits)),
            dma((waves, splits)),
            dma((waves, splits)),
            dma((waves, splits)),
            dma((waves, splits)),
            dma((2,)),
            dma((2,)),
            dma((waves, splits)),
        ],
        compiler_params=pltpu.CompilerParams(
            collective_id=0, has_side_effects=True, vmem_limit_bytes=VMEM_LIMIT
        ),
        name="chain",
    )(
        right_side[0].reshape(waves, WAVE, local),
        diag_inverse[0],
        lower_blocks[0],
        block_pattern[0],
    )
    solved, update = pl.pallas_call(
        place,
        out_shape=(shape, shape),
        in_specs=[VMEM, VMEM],
        out_specs=(ANY, ANY),
        scratch_shapes=[dma((2,))],
        name="place",
    )(solved, update)
    return solved.reshape(1, sources, local), update.reshape(1, sources, local)


def solution(mesh):
    return jax.shard_map(
        functools.partial(on_device, mesh.shape["leaf"], mesh.shape["rows"]),
        mesh=mesh,
        in_specs=(
            P("leaf", None, "rows"),
            P("leaf", "rows", None),
            P("leaf", "rows", None),
            P("leaf", "rows", None),
        ),
        out_specs=(P("leaf", None, "rows"), P("leaf", None, "rows")),
        check_vma=False,
    )
```

```python
import functools

import jax
import jax.numpy as jnp
from jax import lax
from jax.experimental import pallas as pl
from jax.experimental.pallas import tpu as pltpu
from jax.sharding import PartitionSpec as P

MESH = pl.DeviceIdType.MESH
WAVE = 8
AHEAD = 1
FIRST_AHEAD = 1
EARLY = 3
HELPER = 2
VMEM_LIMIT = 54_000_000
PLACE_LIMIT = 4_000_000
LANES = 128


def partner(place, step, size):
    if size & (size - 1):
        return (place + step) % size
    result, bit = 0, 1
    while bit < size:
        result = result + ((place // bit + step // bit) % 2) * bit
        bit *= 2
    return result


def halves(x):
    high = x.astype(jnp.bfloat16)
    low = (x - high.astype(jnp.float32)).astype(jnp.bfloat16)
    return high, low


def kernel(
    groups, splits, right_ref, inverse_hbm, lower_hbm, pattern_ref, solved_ref, update_ref,
    inverse_stage, lower_stage, inverse_parts, lower_parts, arriving, gathered, leaving, next_right, detour,
    inverse_sem, lower_sem, arriving_sem, gathered_sem, first_sem, leaving_sem, spread_sem, right_sem, detour_sem, passed_sem,
):
    g = lax.axis_index("leaf")
    z = lax.axis_index("rows")
    waves, size, local = right_ref.shape
    width = pattern_ref.shape[1]
    pieces = inverse_sem.shape[0]
    piece = local // pieces
    total = splits * local
    helped = groups > HELPER and splits > 1 and waves > EARLY
    direct = EARLY if helped else waves
    ahead = AHEAD + (FIRST_AHEAD - AHEAD) * (1 - jnp.minimum(g, 1))

    def piece_copies(source, stage, sems):
        return [
            pltpu.make_async_copy(
                source.at[pl.ds(i * piece, piece)], stage.at[pl.ds(i * piece, piece)], sems.at[i]
            )
            for i in range(pieces)
        ]

    inverse_copies = piece_copies(inverse_hbm, inverse_stage, inverse_sem)
    lower_copies = piece_copies(lower_hbm, lower_stage, lower_sem)
    for copy in inverse_copies:
        copy.start()

    barrier = pltpu.get_barrier_semaphore()

    def greet(leaf, row):
        pl.semaphore_signal(
            barrier, inc=1, device_id={"leaf": leaf, "rows": row}, device_id_type=MESH
        )

    for j in range(1, splits):
        greet(g, partner(z, j, splits))

    @pl.when(g > 0)
    def _():
        for j in range(splits):
            greet(g - 1, partner(z, j, splits))

    @pl.when(g < groups - 1)
    def _():
        for j in range(splits):
            greet(g + 1, partner(z, j, splits))

    neighbours = jnp.minimum(g, 1) + jnp.minimum(groups - 1 - g, 1)
    if helped:
        for one, other in ((0, HELPER), (HELPER, 0)):
            @pl.when(g == one)
            def _(other=other):
                for j in range(splits):
                    greet(other, partner(z, j, splits))

        neighbours = neighbours + jnp.where((g == 0) | (g == HELPER), 1, 0)
    pl.semaphore_wait(barrier, splits - 1 + splits * neighbours)

    def right_copy():
        return pltpu.make_async_remote_copy(
            src_ref=right_ref, dst_ref=next_right, send_sem=right_sem.at[0],
            recv_sem=right_sem.at[1], device_id={"leaf": g - 1, "rows": z}, device_id_type=MESH,
        )

    def first_copy(k, j):
        return pltpu.make_async_remote_copy(
            src_ref=right_ref.at[k], dst_ref=arriving.at[k, z], send_sem=first_sem.at[k, j],
            recv_sem=arriving_sem.at[k, z],
            device_id={"leaf": g, "rows": partner(z, j, splits)}, device_id_type=MESH,
        )

    def own_copy(k):
        return pltpu.make_async_copy(right_ref.at[k], arriving.at[k, z], arriving_sem.at[k, z])

    def onward_copy(k, j):
        return pltpu.make_async_remote_copy(
            src_ref=leaving.at[k], dst_ref=arriving.at[k, z], send_sem=leaving_sem.at[k, j],
            recv_sem=arriving_sem.at[k, z],
            device_id={"leaf": g + 1, "rows": partner(z, j, splits)}, device_id_type=MESH,
        )

    def spread_copy(k, j):
        return pltpu.make_async_remote_copy(
            src_ref=gathered.at[k, z], dst_ref=gathered.at[k, z], send_sem=spread_sem.at[k, j],
            recv_sem=gathered_sem.at[k, z],
            device_id={"leaf": g, "rows": partner(z, j, splits)}, device_id_type=MESH,
        )

    def detour_copy():
        rest = pl.ds(direct, waves - direct)
        return pltpu.make_async_remote_copy(
            src_ref=right_ref.at[rest], dst_ref=detour.at[rest], send_sem=detour_sem.at[0],
            recv_sem=detour_sem.at[1], device_id={"leaf": HELPER, "rows": z}, device_id_type=MESH,
        )

    def passed_copy(k, j):
        return pltpu.make_async_remote_copy(
            src_ref=detour.at[k], dst_ref=arriving.at[k, z], send_sem=passed_sem.at[k, j],
            recv_sem=arriving_sem.at[k, z],
            device_id={"leaf": 0, "rows": partner(z, j, splits)}, device_id_type=MESH,
        )

    @pl.when(g == 0)
    def _():
        def direct_sends(k, _):
            for j in range(splits - 1, 0, -1):
                first_copy(k, j).start()
            return 0

        def own_sends(k, _):
            own_copy(k).start()
            return 0

        direct_sends(0, 0)
        own_copy(0).start()
        if helped:
            detour_copy().start()
        lax.fori_loop(1, direct, direct_sends, 0)
        lax.fori_loop(1, waves, own_sends, 0)

    @pl.when(g > 0)
    def _():
        right_copy().start()

    def store_turned(parts, rows, q, values):
        high, low = halves(values.T)
        parts[q, :, pl.ds(rows, piece)] = high
        parts[q, :, pl.ds(local + rows, piece)] = low

    def prepare_inverse():
        for i in range(pieces):
            inverse_copies[i].wait()
            lower_copies[i].start()
            for q in range(splits):
                store_turned(
                    inverse_parts, i * piece, q,
                    inverse_stage[pl.ds(i * piece, piece), pl.ds(q * local, local)],
                )

    def prepare_lower():
        block = total // width
        row = lax.broadcasted_iota(jnp.int32, (width, total), 0)
        column = lax.broadcasted_iota(jnp.int32, (width, total), 1)
        spread = jnp.where(column // block == row, 1.0, 0.0).astype(jnp.bfloat16)
        mask = jnp.dot(
            pattern_ref[...].astype(jnp.float32).astype(jnp.bfloat16), spread,
            preferred_element_type=jnp.float32,
        )
        for i in range(pieces):
            lower_copies[i].wait()
            for q in range(splits):
                kept = [
                    lower_stage[pl.ds(h * block, block), pl.ds(q * local, local)]
                    * mask[h : h + 1, q * local : (q + 1) * local]
                    for h in range(i * piece // block, (i + 1) * piece // block)
                ]
                store_turned(lower_parts, i * piece, q, jnp.concatenate(kept, 0))

    def product(x, parts):
        high, low = halves(x)
        out = lax.dot_general(
            jnp.concatenate([high, low], 0), parts, (((1,), (0,)), ((), ())),
            preferred_element_type=jnp.float32,
        )
        return (out[:size, :local] + (out[size:, :local] + out[:size, local:])) + out[size:, local:]

    def solve(k):
        result = None
        for j in range(splits):
            q = partner(z, j, splits)
            pltpu.make_async_copy(arriving.at[k, q], arriving.at[k, q], arriving_sem.at[k, q]).wait()
            term = product(arriving[k, q], inverse_parts[q])
            result = term if result is None else result + term
        gathered[k, z] = result
        for j in range(splits - 1, 0, -1):
            spread_copy(k, j).start()
        solved_ref[k] = result

    def push(k):
        result = None
        for j in range(splits):
            q = partner(z, j, splits)
            if j:
                pltpu.make_async_copy(gathered.at[k, q], gathered.at[k, q], gathered_sem.at[k, q]).wait()
            term = product(gathered[k, q], lower_parts[q])
            result = term if result is None else result + term

        @pl.when(g < groups - 1)
        def _():
            leaving[k] = next_right[k] - result
            for j in range(splits - 1, -1, -1):
                onward_copy(k, j).start()

        update_ref[k] = result

    prepare_inverse()

    if helped:
        @pl.when(g == HELPER)
        def _():
            detour_copy().wait_recv()

            def pass_on(k, _):
                for j in range(splits - 1, 0, -1):
                    passed_copy(k, j).start()
                return 0

            lax.fori_loop(direct, waves, pass_on, 0)

    @pl.when(g > 0)
    def _():
        prepare_lower()

    def section(k, _):
        @pl.when(k < waves)
        def _():
            solve(k)

        @pl.when((k == 0) & (g == 0))
        def _():
            prepare_lower()

        @pl.when((k == ahead) & (g < groups - 1))
        def _():
            right_copy().wait_recv()

        @pl.when(k >= ahead)
        def _():
            push(k - ahead)

        return 0

    lax.fori_loop(0, waves + ahead, section, 0)

    def finish(k, _):
        for j in range(1, splits):
            spread_copy(k, j).wait_send()

        @pl.when((g == 0) & (k < direct))
        def _():
            for j in range(1, splits):
                first_copy(k, j).wait_send()

        if helped:
            @pl.when((g == HELPER) & (k >= direct))
            def _():
                for j in range(1, splits):
                    passed_copy(k, j).wait_send()

        @pl.when(g < groups - 1)
        def _():
            for j in range(splits):
                onward_copy(k, j).wait_send()

        return 0

    lax.fori_loop(0, waves, finish, 0)

    @pl.when(g > 0)
    def _():
        right_copy().wait_send()

    if helped:
        @pl.when(g == 0)
        def _():
            detour_copy().wait_send()


def place(solved_ref, update_ref, solved_hbm, update_hbm, sems):
    copies = [
        pltpu.make_async_copy(solved_ref, solved_hbm, sems.at[0]),
        pltpu.make_async_copy(update_ref, update_hbm, sems.at[1]),
    ]
    for copy in copies:
        copy.start()
    for copy in copies:
        copy.wait()


def on_device(groups, splits, right_side, diag_inverse, lower_blocks, block_pattern):
    _, sources, local = right_side.shape
    total = diag_inverse.shape[2]
    pieces = local // LANES
    waves = sources // WAVE
    VMEM = pl.BlockSpec(memory_space=pltpu.VMEM)
    ANY = pl.BlockSpec(memory_space=pl.ANY)
    shape = jax.ShapeDtypeStruct((waves, WAVE, local), jnp.float32)
    dma = pltpu.SemaphoreType.DMA
    solved, update = pl.pallas_call(
        functools.partial(kernel, groups, splits),
        out_shape=(shape, shape),
        in_specs=[VMEM, ANY, ANY, VMEM],
        out_specs=(VMEM, VMEM),
        scratch_shapes=[
            pltpu.VMEM((local, total), jnp.float32),
            pltpu.VMEM((local, total), jnp.float32),
            pltpu.VMEM((splits, local, 2 * local), jnp.bfloat16),
            pltpu.VMEM((splits, local, 2 * local), jnp.bfloat16),
            pltpu.VMEM((waves, splits, WAVE, local), jnp.float32),
            pltpu.VMEM((waves, splits, WAVE, local), jnp.float32),
            pltpu.VMEM((waves, WAVE, local), jnp.float32),
            pltpu.VMEM((waves, WAVE, local), jnp.float32),
            pltpu.VMEM((waves, WAVE, local), jnp.float32),
            dma((pieces,)),
            dma((pieces,)),
            dma((waves, splits)),
            dma((waves, splits)),
            dma((waves, splits)),
            dma((waves, splits)),
            dma((waves, splits)),
            dma((2,)),
            dma((2,)),
            dma((waves, splits)),
        ],
        compiler_params=pltpu.CompilerParams(
            collective_id=0, has_side_effects=True, vmem_limit_bytes=VMEM_LIMIT
        ),
        name="chain",
    )(
        right_side[0].reshape(waves, WAVE, local),
        diag_inverse[0],
        lower_blocks[0],
        block_pattern[0],
    )
    solved, update = pl.pallas_call(
        place,
        out_shape=(shape, shape),
        in_specs=[VMEM, VMEM],
        out_specs=(ANY, ANY),
        scratch_shapes=[dma((2,))],
        compiler_params=pltpu.CompilerParams(vmem_limit_bytes=PLACE_LIMIT),
        name="place",
    )(solved, update)
    return solved.reshape(1, sources, local), update.reshape(1, sources, local)


def solution(mesh):
    return jax.shard_map(
        functools.partial(on_device, mesh.shape["leaf"], mesh.shape["rows"]),
        mesh=mesh,
        in_specs=(
            P("leaf", None, "rows"),
            P("leaf", "rows", None),
            P("leaf", "rows", None),
            P("leaf", "rows", None),
        ),
        out_specs=(P("leaf", None, "rows"), P("leaf", None, "rows")),
        check_vma=False,
    )
```

```python
import functools

import jax
import jax.numpy as jnp
from jax import lax
from jax.experimental import pallas as pl
from jax.experimental.pallas import tpu as pltpu
from jax.sharding import PartitionSpec as P

MESH = pl.DeviceIdType.MESH
WAVE = 8
AHEAD = 1
FIRST_AHEAD = 1
EARLY = 3
HELPER = 2
VMEM_LIMIT = 56_000_000
PLACE_LIMIT = 4_000_000
LANES = 128


def partner(place, step, size):
    if size & (size - 1):
        return (place + step) % size
    result, bit = 0, 1
    while bit < size:
        result = result + ((place // bit + step // bit) % 2) * bit
        bit *= 2
    return result


def halves(x):
    high = x.astype(jnp.bfloat16)
    low = (x - high.astype(jnp.float32)).astype(jnp.bfloat16)
    return high, low


def kernel(
    groups, splits, right_ref, inverse_hbm, lower_hbm, pattern_ref, solved_ref, update_ref,
    inverse_stage, lower_stage, inverse_parts, lower_parts, arriving, gathered, leaving, next_right, detour,
    inverse_sem, lower_sem, arriving_sem, gathered_sem, first_sem, leaving_sem, spread_sem, right_sem, detour_sem, passed_sem,
):
    g = lax.axis_index("leaf")
    z = lax.axis_index("rows")
    waves, size, local = right_ref.shape
    width = pattern_ref.shape[1]
    pieces = inverse_sem.shape[0]
    piece = local // pieces
    total = splits * local
    helped = groups > HELPER and splits > 1 and waves > EARLY
    direct = EARLY if helped else waves
    ahead = AHEAD + (FIRST_AHEAD - AHEAD) * (1 - jnp.minimum(g, 1))

    def piece_copies(source, stage, sems):
        return [
            pltpu.make_async_copy(
                source.at[pl.ds(i * piece, piece)], stage.at[pl.ds(i * piece, piece)], sems.at[i]
            )
            for i in range(pieces)
        ]

    inverse_copies = piece_copies(inverse_hbm, inverse_stage, inverse_sem)
    lower_copies = piece_copies(lower_hbm, lower_stage, lower_sem)
    for copy in inverse_copies:
        copy.start()

    barrier = pltpu.get_barrier_semaphore()

    def greet(leaf, row):
        pl.semaphore_signal(
            barrier, inc=1, device_id={"leaf": leaf, "rows": row}, device_id_type=MESH
        )

    for j in range(1, splits):
        greet(g, partner(z, j, splits))

    @pl.when(g > 0)
    def _():
        for j in range(splits):
            greet(g - 1, partner(z, j, splits))

    @pl.when(g < groups - 1)
    def _():
        for j in range(splits):
            greet(g + 1, partner(z, j, splits))

    neighbours = jnp.minimum(g, 1) + jnp.minimum(groups - 1 - g, 1)
    if helped:
        for one, other in ((0, HELPER), (HELPER, 0)):
            @pl.when(g == one)
            def _(other=other):
                for j in range(splits):
                    greet(other, partner(z, j, splits))

        neighbours = neighbours + jnp.where((g == 0) | (g == HELPER), 1, 0)
    pl.semaphore_wait(barrier, splits - 1 + splits * neighbours)

    def right_copy():
        return pltpu.make_async_remote_copy(
            src_ref=right_ref, dst_ref=next_right, send_sem=right_sem.at[0],
            recv_sem=right_sem.at[1], device_id={"leaf": g - 1, "rows": z}, device_id_type=MESH,
        )

    def first_copy(k, j):
        return pltpu.make_async_remote_copy(
            src_ref=right_ref.at[k], dst_ref=arriving.at[k, z], send_sem=first_sem.at[k, j],
            recv_sem=arriving_sem.at[k, z],
            device_id={"leaf": g, "rows": partner(z, j, splits)}, device_id_type=MESH,
        )

    def own_copy(k):
        return pltpu.make_async_copy(right_ref.at[k], arriving.at[k, z], arriving_sem.at[k, z])

    def onward_copy(k, j):
        return pltpu.make_async_remote_copy(
            src_ref=leaving.at[k], dst_ref=arriving.at[k, z], send_sem=leaving_sem.at[k, j],
            recv_sem=arriving_sem.at[k, z],
            device_id={"leaf": g + 1, "rows": partner(z, j, splits)}, device_id_type=MESH,
        )

    def spread_copy(k, j):
        return pltpu.make_async_remote_copy(
            src_ref=gathered.at[k, z], dst_ref=gathered.at[k, z], send_sem=spread_sem.at[k, j],
            recv_sem=gathered_sem.at[k, z],
            device_id={"leaf": g, "rows": partner(z, j, splits)}, device_id_type=MESH,
        )

    def detour_copy():
        rest = pl.ds(direct, waves - direct)
        return pltpu.make_async_remote_copy(
            src_ref=right_ref.at[rest], dst_ref=detour.at[rest], send_sem=detour_sem.at[0],
            recv_sem=detour_sem.at[1], device_id={"leaf": HELPER, "rows": z}, device_id_type=MESH,
        )

    def passed_copy(k, j):
        return pltpu.make_async_remote_copy(
            src_ref=detour.at[k], dst_ref=arriving.at[k, z], send_sem=passed_sem.at[k, j],
            recv_sem=arriving_sem.at[k, z],
            device_id={"leaf": 0, "rows": partner(z, j, splits)}, device_id_type=MESH,
        )

    @pl.when(g == 0)
    def _():
        def direct_sends(k, _):
            for j in range(splits - 1, 0, -1):
                first_copy(k, j).start()
            return 0

        def own_sends(k, _):
            own_copy(k).start()
            return 0

        direct_sends(0, 0)
        own_copy(0).start()
        if helped:
            detour_copy().start()
        lax.fori_loop(1, direct, direct_sends, 0)
        lax.fori_loop(1, waves, own_sends, 0)

    @pl.when(g > 0)
    def _():
        right_copy().start()

    def store_turned(parts, rows, q, values):
        high, low = halves(values.T)
        parts[q, :, pl.ds(rows, piece)] = high
        parts[q, :, pl.ds(local + rows, piece)] = low

    def prepare_inverse():
        for i in range(pieces):
            inverse_copies[i].wait()
            lower_copies[i].start()
            for q in range(splits):
                store_turned(
                    inverse_parts, i * piece, q,
                    inverse_stage[pl.ds(i * piece, piece), pl.ds(q * local, local)],
                )

    def prepare_lower():
        block = total // width
        row = lax.broadcasted_iota(jnp.int32, (width, total), 0)
        column = lax.broadcasted_iota(jnp.int32, (width, total), 1)
        spread = jnp.where(column // block == row, 1.0, 0.0).astype(jnp.bfloat16)
        mask = jnp.dot(
            pattern_ref[...].astype(jnp.float32).astype(jnp.bfloat16), spread,
            preferred_element_type=jnp.float32,
        )
        for i in range(pieces):
            lower_copies[i].wait()
            for q in range(splits):
                kept = [
                    lower_stage[pl.ds(h * block, block), pl.ds(q * local, local)]
                    * mask[h : h + 1, q * local : (q + 1) * local]
                    for h in range(i * piece // block, (i + 1) * piece // block)
                ]
                store_turned(lower_parts, i * piece, q, jnp.concatenate(kept, 0))

    def product(x, parts):
        high, low = halves(x)
        out = lax.dot_general(
            jnp.concatenate([high, low], 0), parts, (((1,), (0,)), ((), ())),
            preferred_element_type=jnp.float32,
        )
        return (out[:size, :local] + (out[size:, :local] + out[:size, local:])) + out[size:, local:]

    def solve(k):
        result = None
        for j in range(splits):
            q = partner(z, j, splits)
            pltpu.make_async_copy(arriving.at[k, q], arriving.at[k, q], arriving_sem.at[k, q]).wait()
            term = product(arriving[k, q], inverse_parts[q])
            result = term if result is None else result + term
        gathered[k, z] = result
        for j in range(splits - 1, 0, -1):
            spread_copy(k, j).start()
        solved_ref[k] = result

    def push(k):
        result = None
        for j in range(splits):
            q = partner(z, j, splits)
            if j:
                pltpu.make_async_copy(gathered.at[k, q], gathered.at[k, q], gathered_sem.at[k, q]).wait()
            term = product(gathered[k, q], lower_parts[q])
            result = term if result is None else result + term

        @pl.when(g < groups - 1)
        def _():
            leaving[k] = next_right[k] - result
            for j in range(splits - 1, -1, -1):
                onward_copy(k, j).start()

        update_ref[k] = result

    prepare_inverse()

    if helped:
        @pl.when(g == HELPER)
        def _():
            detour_copy().wait_recv()

            def pass_on(k, _):
                for j in range(splits - 1, 0, -1):
                    passed_copy(k, j).start()
                return 0

            lax.fori_loop(direct, waves, pass_on, 0)

    @pl.when(g > 0)
    def _():
        prepare_lower()

    def section(k, _):
        @pl.when(k < waves)
        def _():
            solve(k)

        @pl.when((k == 0) & (g == 0))
        def _():
            prepare_lower()

        @pl.when((k == ahead) & (g < groups - 1))
        def _():
            right_copy().wait_recv()

        @pl.when(k >= ahead)
        def _():
            push(k - ahead)

        return 0

    lax.fori_loop(0, waves + ahead, section, 0)

    def finish(k, _):
        for j in range(1, splits):
            spread_copy(k, j).wait_send()

        @pl.when((g == 0) & (k < direct))
        def _():
            for j in range(1, splits):
                first_copy(k, j).wait_send()

        if helped:
            @pl.when((g == HELPER) & (k >= direct))
            def _():
                for j in range(1, splits):
                    passed_copy(k, j).wait_send()

        @pl.when(g < groups - 1)
        def _():
            for j in range(splits):
                onward_copy(k, j).wait_send()

        return 0

    lax.fori_loop(0, waves, finish, 0)

    @pl.when(g > 0)
    def _():
        right_copy().wait_send()

    if helped:
        @pl.when(g == 0)
        def _():
            detour_copy().wait_send()


def place(solved_ref, update_ref, solved_hbm, update_hbm, sems):
    copies = [
        pltpu.make_async_copy(solved_ref, solved_hbm, sems.at[0]),
        pltpu.make_async_copy(update_ref, update_hbm, sems.at[1]),
    ]
    for copy in copies:
        copy.start()
    for copy in copies:
        copy.wait()


def on_device(groups, splits, right_side, diag_inverse, lower_blocks, block_pattern):
    _, sources, local = right_side.shape
    total = diag_inverse.shape[2]
    pieces = local // LANES
    waves = sources // WAVE
    VMEM = pl.BlockSpec(memory_space=pltpu.VMEM)
    ANY = pl.BlockSpec(memory_space=pl.ANY)
    shape = jax.ShapeDtypeStruct((waves, WAVE, local), jnp.float32)
    dma = pltpu.SemaphoreType.DMA
    solved, update = pl.pallas_call(
        functools.partial(kernel, groups, splits),
        out_shape=(shape, shape),
        in_specs=[ANY, ANY, ANY, VMEM],
        out_specs=(VMEM, VMEM),
        scratch_shapes=[
            pltpu.VMEM((local, total), jnp.float32),
            pltpu.VMEM((local, total), jnp.float32),
            pltpu.VMEM((splits, local, 2 * local), jnp.bfloat16),
            pltpu.VMEM((splits, local, 2 * local), jnp.bfloat16),
            pltpu.VMEM((waves, splits, WAVE, local), jnp.float32),
            pltpu.VMEM((waves, splits, WAVE, local), jnp.float32),
            pltpu.VMEM((waves, WAVE, local), jnp.float32),
            pltpu.VMEM((waves, WAVE, local), jnp.float32),
            pltpu.VMEM((waves, WAVE, local), jnp.float32),
            dma((pieces,)),
            dma((pieces,)),
            dma((waves, splits)),
            dma((waves, splits)),
            dma((waves, splits)),
            dma((waves, splits)),
            dma((waves, splits)),
            dma((2,)),
            dma((2,)),
            dma((waves, splits)),
        ],
        compiler_params=pltpu.CompilerParams(
            collective_id=0, has_side_effects=True, vmem_limit_bytes=VMEM_LIMIT
        ),
        name="chain",
    )(
        right_side[0].reshape(waves, WAVE, local),
        diag_inverse[0],
        lower_blocks[0],
        block_pattern[0],
    )
    solved, update = pl.pallas_call(
        place,
        out_shape=(shape, shape),
        in_specs=[VMEM, VMEM],
        out_specs=(ANY, ANY),
        scratch_shapes=[dma((2,))],
        compiler_params=pltpu.CompilerParams(vmem_limit_bytes=PLACE_LIMIT),
        name="place",
    )(solved, update)
    return solved.reshape(1, sources, local), update.reshape(1, sources, local)


def solution(mesh):
    return jax.shard_map(
        functools.partial(on_device, mesh.shape["leaf"], mesh.shape["rows"]),
        mesh=mesh,
        in_specs=(
            P("leaf", None, "rows"),
            P("leaf", "rows", None),
            P("leaf", "rows", None),
            P("leaf", "rows", None),
        ),
        out_specs=(P("leaf", None, "rows"), P("leaf", None, "rows")),
        check_vma=False,
    )
```
